512 devices in a mesh: view: 32 (over x_lo, z), row: 16 (over x_hi, y, core).
Axes of the slice: x: 4 (x_hi: 2, x_lo: 2; x = x_hi * 2 + x_lo), y: 4, z: 16, core: 2. Of those that a mesh axis runs over, the one named last changes fastest.
Arguments:
- light_field: float32 [256, 64, 1920], P('view', 'row'), may hold values from -6 to 6
Outputs:
- refined_disparity: float32 [256, 64, 1920], P('view', 'row')
The draws below stay inside these ranges and needn't reach their ends.
All inputs are finite; a program needn't handle non-finite values.
Results may differ from the reference program's by a relative error of at most 0.00002.
Values sent between devices are 32-bit elements; how exact they have to be, the bound alone decides.
A program may use at most 128 MiB of HBM per device.

```python
import math
import jax
import jax.numpy as jnp
from jax import lax

U = 16
V = 16
X = 1920
Y = 64


def levels(rng, shape, cuts, low, high):
    gain, own = 1.0, jax.random.fold_in(rng, 6)
    for axis_at, parts in cuts:
        draws = jnp.exp(jax.random.uniform(jax.random.fold_in(own, axis_at), (parts,), jnp.float32, low / len(cuts), high / len(cuts)))
        gain = gain * jnp.repeat(draws, shape[axis_at] // parts).reshape([-1 if axis == axis_at else 1 for axis in range(len(shape))])
    return gain


def bell_draw(key, dims, deviation, reach, cuts=(), kind=jnp.bfloat16):
    loudness = levels(key, dims, cuts, -0.22, 0.18) if cuts else 1.0
    result = jax.random.normal(key, dims, jnp.float32) * deviation * loudness
    return jnp.minimum(jnp.maximum(result, -reach), reach).astype(kind)


def setup_inputs(seed: int = 0) -> dict:
    arg_keys = jax.random.split(jax.random.key(seed), 2)
    return {
        "light_field": bell_draw(arg_keys[0], (U * V, Y, X), 1.0, 6.0, ((0, 32), (1, 16)), jnp.float32),
    }


TENSOR_DAMPING = 0.1
COHERENCE_DAMPING = 0.1
CONFIDENCE_FLOOR = 0.05
SPATIAL_SPREAD = 8.0
RANGE_SPREAD = 2.0


def shifted(source, dimension, offset, length):
    return lax.slice_in_dim(source, offset, offset + length, axis=dimension)


def derivative(source, dimension):
    length = source.shape[dimension] - 2
    return 0.5 * (shifted(source, dimension, 2, length) - shifted(source, dimension, 0, length))


def smooth_three(source, dimension):
    length = source.shape[dimension] - 2
    return 0.25 * (shifted(source, dimension, 0, length) + 2.0 * shifted(source, dimension, 1, length) + shifted(source, dimension, 2, length))


def smooth_five(source, dimension):
    length = source.shape[dimension] - 4
    return 0.0625 * (shifted(source, dimension, 0, length) + 4.0 * shifted(source, dimension, 1, length) + 6.0 * shifted(source, dimension, 2, length) + 4.0 * shifted(source, dimension, 3, length) + shifted(source, dimension, 4, length))


def slice_estimate(padded, angle_dim, space_dim):
    grad_space = derivative(padded, space_dim)
    grad_space = shifted(grad_space, angle_dim, 1, grad_space.shape[angle_dim] - 2)
    grad_angle = derivative(padded, angle_dim)
    grad_angle = shifted(grad_angle, space_dim, 1, grad_angle.shape[space_dim] - 2)

    def blurred(source):
        return smooth_five(smooth_three(source, angle_dim), space_dim)

    space_space = blurred(grad_space * grad_space)
    space_angle = blurred(grad_space * grad_angle)
    angle_angle = blurred(grad_angle * grad_angle)
    disparity = -space_angle / (space_space + TENSOR_DAMPING)
    spread = angle_angle - space_space
    total_energy = angle_angle + space_space
    coherence = (spread * spread + 4.0 * space_angle * space_angle) / (total_energy * total_energy + COHERENCE_DAMPING)
    return disparity, coherence


def view_estimates(with_columns, with_rows):
    with_columns = jnp.pad(with_columns, ((0, 0), (2, 2), (0, 0), (0, 0)))
    with_rows = jnp.pad(with_rows, ((2, 2), (0, 0), (0, 0), (0, 0)))
    horizontal_disp, horizontal_conf = slice_estimate(with_columns, 1, 3)
    vertical_disp, vertical_conf = slice_estimate(with_rows, 0, 2)
    merged = (horizontal_conf * horizontal_disp + vertical_conf * vertical_disp) / (horizontal_conf + vertical_conf + CONFIDENCE_FLOOR)
    weight = CONFIDENCE_FLOOR + 0.5 * (horizontal_conf + vertical_conf)
    return merged, weight


def joint_filter(guidance, estimate, weight, row_count, col_count):
    centre = guidance[:, 3:3 + row_count, 3:3 + col_count]
    accumulated = jnp.zeros(centre.shape, jnp.float32)
    norm_sum = jnp.zeros(centre.shape, jnp.float32)
    for row_step in range(7):
        for col_step in range(7):
            nearby = guidance[:, row_step:row_step + row_count, col_step:col_step + col_count]
            difference = nearby - centre
            distance = float((row_step - 3) * (row_step - 3) + (col_step - 3) * (col_step - 3)) / SPATIAL_SPREAD
            factor = jnp.exp(-distance - difference * difference / RANGE_SPREAD) * weight[:, row_step:row_step + row_count, col_step:col_step + col_count]
            accumulated = accumulated + factor * estimate[:, row_step:row_step + row_count, col_step:col_step + col_count]
            norm_sum = norm_sum + factor
    return accumulated / norm_sum


def reference(light_field):
    luminance = light_field.reshape(U, V, Y, X)
    padded = jnp.pad(luminance, ((0, 0), (0, 0), (3, 3), (3, 3)))
    block_width = math.gcd(X, 128)
    starts = jnp.arange(X // block_width, dtype=jnp.int32) * block_width

    def estimate_block(offset):
        column_block = lax.dynamic_slice_in_dim(padded, offset, block_width + 6, axis=3)
        with_columns = column_block[:, :, 3:3 + Y, :]
        with_rows = column_block[:, :, :, 3:3 + block_width]
        return view_estimates(with_columns, with_rows)

    merged, weight = lax.map(estimate_block, starts)
    merged = merged.transpose(1, 2, 3, 0, 4).reshape(U, V, Y, X)
    weight = weight.transpose(1, 2, 3, 0, 4).reshape(U, V, Y, X)
    border = ((0, 0), (0, 0), (3, 3), (3, 3))
    merged_pad = jnp.pad(merged, border)
    weight_pad = jnp.pad(weight, border)

    def filter_group(group):
        guidance, estimate, weights = group
        return joint_filter(guidance, estimate, weights, Y, X)

    refined = lax.map(filter_group, (padded, merged_pad, weight_pad))
    return refined.reshape(U * V, Y, X)
```

```python
import functools
import math

import jax
import jax.numpy as jnp
from jax import lax
from jax.experimental import pallas as pl
from jax.experimental.pallas import tpu as pltpu
from jax.sharding import PartitionSpec as P

DAMPING = 0.1
FLOOR = 0.05
LANES = 128
LOG2E = 1.4426950408889634
RANGE_SCALE = math.sqrt(LOG2E / 2.0)
MESH = pl.DeviceIdType.MESH


def moved(value, offset):
    if offset == 0:
        return value
    width = value.shape[-1]
    return pltpu.roll(value, (-offset) % width, value.ndim - 1)


def tensor_terms(space, angle):
    terms = []
    for left, right in ((space, space), (space, angle), (angle, angle)):
        a, b, c = (x * y for x, y in zip(left, right))
        terms.append((a + c) + 2.0 * b)
    return terms


def five(m2, m1, c0, p1, p2):
    return (m2 + p2) + 4.0 * (m1 + p1) + 6.0 * c0


def disparity_confidence(ss, sa, aa):
    disparity = -sa / (ss + DAMPING)
    spread = aa - ss
    total = aa + ss
    confidence = (spread * spread + 4.0 * sa * sa) / (total * total + DAMPING)
    return disparity, confidence


def kernel(chunks, x_ref, xv_ref, out_ref, lum, pair, wide, horiz, mw, moved_ref, *sems):
    n_row = lax.axis_size("row")
    n_u = lax.axis_size("view") // 2
    d = lax.axis_index("view")
    r = lax.axis_index("row")
    u = d // 2
    h = lax.rem(d, 2)
    rows, _, width = x_ref.shape
    padded = width + 2 * LANES
    step = width // chunks
    inner = slice(LANES, LANES + width)

    up = u < n_u - 1
    down = u > 0
    both = jnp.logical_and(up, down)
    row_up = r < n_row - 1
    row_down = r > 0
    always = d >= 0
    held = (u >= 2, down, always, up, u < n_u - 2)
    to_up = {"view": d + 2}
    to_down = {"view": d - 2}
    to_pair = {"view": d + 1 - 2 * h}
    to_row_up = {"row": r + 1}
    to_row_down = {"row": r - 1}

    send_sems, recv_sems = sems
    used = [0]

    def copy(src, dst, device, sends, receives):
        i = used[0]
        used[0] += 1
        c = pltpu.make_async_remote_copy(
            src_ref=src, dst_ref=dst, send_sem=send_sems.at[i], recv_sem=recv_sems.at[i],
            device_id=device, device_id_type=MESH,
        )
        return c, sends, receives

    def start(item):
        pl.when(item[1])(item[0].start)

    def arrived(item):
        pl.when(item[2])(item[0].wait_recv)

    def left(item):
        pl.when(item[1])(item[0].wait_send)

    barrier = pltpu.get_barrier_semaphore()
    peers = ((up, to_up), (down, to_down), (always, to_pair), (row_up, to_row_up), (row_down, to_row_down))
    count = jnp.int32(0)
    for cond, device in peers:
        @pl.when(cond)
        def _(device=device):
            pl.semaphore_signal(barrier, inc=1, device_id=device, device_id_type=MESH)
        count = count + cond.astype(jnp.int32)
    pl.semaphore_wait(barrier, count)

    def cols(c):
        return pl.ds(LANES + c * step, step)

    near, far, edge, merged_edge = {}, {}, {}, {}
    all_copies = []
    pair_copy = copy(xv_ref.at[pl.ds(6 * (1 - h), 2)], pair, to_pair, always, always)
    all_copies.append(pair_copy)
    for c in range(chunks):
        own = x_ref.at[:, :, pl.ds(c * step, step)]
        near[c] = (
            copy(own, lum.at[1, pl.ds(3, rows), :, cols(c)], to_up, up, down),
            copy(own, lum.at[3, pl.ds(3, rows), :, cols(c)], to_down, down, up),
        )
        far[c] = (
            copy(lum.at[1, pl.ds(3, rows), :, cols(c)], lum.at[0, pl.ds(3, rows), :, cols(c)], to_up, both, held[0]),
            copy(lum.at[3, pl.ds(3, rows), :, cols(c)], lum.at[4, pl.ds(3, rows), :, cols(c)], to_down, both, held[4]),
        )
        all_copies += [*near[c], *far[c]]
        for k in range(5):
            if k == 2:
                high = x_ref.at[pl.ds(rows - 3, 3), :, pl.ds(c * step, step)]
                low = x_ref.at[pl.ds(0, 3), :, pl.ds(c * step, step)]
            else:
                high = lum.at[k, pl.ds(rows, 3), :, cols(c)]
                low = lum.at[k, pl.ds(3, 3), :, cols(c)]
            here = held[k]
            edge[c, k] = (
                copy(high, lum.at[k, pl.ds(0, 3), :, cols(c)], to_row_up,
                     jnp.logical_and(here, row_up), jnp.logical_and(here, row_down)),
                copy(low, lum.at[k, pl.ds(3 + rows, 3), :, cols(c)], to_row_down,
                     jnp.logical_and(here, row_down), jnp.logical_and(here, row_up)),
            )
            all_copies += [*edge[c, k]]
        merged_edge[c] = (
            copy(mw.at[:, pl.ds(rows, 3), :, cols(c)], mw.at[:, pl.ds(0, 3), :, cols(c)], to_row_up, row_up, row_down),
            copy(mw.at[:, pl.ds(3, 3), :, cols(c)], mw.at[:, pl.ds(3 + rows, 3), :, cols(c)], to_row_down, row_down, row_up),
        )
        all_copies += [*merged_edge[c]]

    start(pair_copy)
    for c in range(chunks):
        for item in near[c]:
            start(item)
    for c in range(chunks):
        for item in edge[c, 2]:
            start(item)

    zero_pad = jnp.zeros((8, LANES), jnp.float32)

    @pl.loop(0, rows + 6)
    def _(i):
        for side in (0, LANES + width):
            lum[2, i, :, side:side + LANES] = zero_pad
            for j in range(2):
                mw[j, i, :, side:side + LANES] = zero_pad

    for k in (0, 1, 3, 4):
        @pl.when(jnp.logical_not(held[k]))
        def _(k=k):
            @pl.loop(0, rows + 6)
            def _(i):
                lum[k, i] = jnp.zeros((8, padded), jnp.float32)

    for cond, first in ((jnp.logical_not(row_down), 0), (jnp.logical_not(row_up), 3 + rows)):
        @pl.when(cond)
        def _(first=first):
            for k in range(5):
                for i in range(first, first + 3):
                    lum[k, i] = jnp.zeros((8, padded), jnp.float32)
            for j in range(2):
                for i in range(first, first + 3):
                    mw[j, i] = jnp.zeros((8, padded), jnp.float32)

    for i in range(rows):
        lum[2, 3 + i, :, inner] = x_ref[i]
        wide[i, 8:16, inner] = x_ref[i]
        for side in (0, LANES + width):
            wide[i, :, side:side + LANES] = jnp.zeros((24, LANES), jnp.float32)
    arrived(pair_copy)
    for i in range(rows):
        for v in range(2):
            value = pair[v, i:i + 1, :]
            wide[i, 6 + v:7 + v, inner] = jnp.where(h == 1, value, 0.0)
            wide[i, 16 + v:17 + v, inner] = jnp.where(h == 0, value, 0.0)

    @pl.loop(0, rows)
    def _(i):
        views = [wide[i, 8 + o:16 + o, :] for o in (-2, -1, 0, 1, 2)]
        space = [moved(views[o], 1) - moved(views[o], -1) for o in (1, 2, 3)]
        angle = [views[o + 1] - views[o - 1] for o in (1, 2, 3)]
        ss, sa, aa = (
            five(*(moved(term, b) for b in (-2, -1, 0, 1, 2)))[:, inner] * (1.0 / 256.0)
            for term in tensor_terms(space, angle)
        )
        disparity, confidence = disparity_confidence(ss, sa, aa)
        horiz[0, i] = confidence * disparity
        horiz[1, i] = confidence

    for c in range(chunks):
        for item, k, on in ((near[c][0], 1, far[c][0]), (near[c][1], 3, far[c][1])):
            arrived(item)
            start(on)
            for e in edge[c, k]:
                start(e)

    for c in range(chunks):
        for e in edge[c, 2]:
            arrived(e)

    @pl.loop(0, rows + 6)
    def _(i):
        value = lum[2, i] * RANGE_SCALE
        for b in range(7):
            moved_ref[b, 0, i] = moved(value, b - 3)[:, inner]

    def vertical(c):
        @pl.loop(0, step // LANES)
        def _(t):
            out_at = pl.multiple_of(c * step + t * LANES, LANES)
            at = pl.multiple_of(out_at + LANES, LANES)
            terms = []
            for i in range(1, rows + 5):
                space = [lum[k, i + 1, :, pl.ds(at, LANES)] - lum[k, i - 1, :, pl.ds(at, LANES)] for k in (1, 2, 3)]
                angle = [lum[k + 1, i, :, pl.ds(at, LANES)] - lum[k - 1, i, :, pl.ds(at, LANES)] for k in (1, 2, 3)]
                terms.append(tensor_terms(space, angle))
            for i in range(rows):
                ss, sa, aa = (
                    five(*(terms[i + j][q] for j in range(5))) * (1.0 / 256.0) for q in range(3)
                )
                disparity, confidence = disparity_confidence(ss, sa, aa)
                product = horiz[0, i, :, pl.ds(out_at, LANES)]
                other = horiz[1, i, :, pl.ds(out_at, LANES)]
                total = other + confidence
                merged = (product + confidence * disparity) / (total + FLOOR)
                weight = FLOOR + 0.5 * total
                mw[0, 3 + i, :, pl.ds(at, LANES)] = merged * weight
                mw[1, 3 + i, :, pl.ds(at, LANES)] = weight

    for c in range(chunks):
        for item, k in ((far[c][0], 0), (far[c][1], 4)):
            arrived(item)
            for e in edge[c, k]:
                start(e)
        if c > 0:
            finish_chunk(c - 1, vertical, edge, merged_edge, arrived, start)
    finish_chunk(chunks - 1, vertical, edge, merged_edge, arrived, start)

    for c in range(chunks):
        for e in merged_edge[c]:
            arrived(e)

    @pl.loop(0, rows + 6)
    def _(i):
        for j in range(2):
            value = mw[j, i]
            for b in range(7):
                moved_ref[b, 1 + j, i] = moved(value, b - 3)[:, inner]

    @pl.loop(0, width // LANES)
    def _(t):
        at = pl.ds(pl.multiple_of(t * LANES, LANES), LANES)
        centre = [moved_ref[3, 0, 3 + i, :, at] for i in range(rows)]
        total = [None] * rows
        norm = [None] * rows
        for b in range(7):
            near_l = [moved_ref[b, 0, i, :, at] for i in range(rows + 6)]
            near_m = [moved_ref[b, 1, i, :, at] for i in range(rows + 6)]
            near_w = [moved_ref[b, 2, i, :, at] for i in range(rows + 6)]
            for i in range(rows):
                for a in range(7):
                    difference = near_l[i + a] - centre[i]
                    distance = ((a - 3) ** 2 + (b - 3) ** 2) / 8.0 * LOG2E
                    e = jnp.exp2(-distance - difference * difference)
                    m = e * near_m[i + a]
                    w = e * near_w[i + a]
                    total[i] = m if total[i] is None else total[i] + m
                    norm[i] = w if norm[i] is None else norm[i] + w
        for i in range(rows):
            out_ref[i, :, at] = total[i] / norm[i]

    for item in all_copies:
        left(item)


def finish_chunk(c, vertical, edge, merged_edge, arrived, start):
    for k in (0, 1, 3, 4):
        for e in edge[c, k]:
            arrived(e)
    vertical(c)
    for e in merged_edge[c]:
        start(e)


def local(light_field):
    views, rows, width = light_field.shape
    tiles = width // LANES
    chunks = 3 if tiles % 3 == 0 else 1
    padded = width + 2 * LANES
    copies = 1 + chunks * 16
    f32 = jnp.float32
    by_row = light_field.transpose(1, 0, 2)
    vmem = pl.BlockSpec(memory_space=pltpu.VMEM)
    refined = pl.pallas_call(
        functools.partial(kernel, chunks),
        out_shape=jax.ShapeDtypeStruct((rows, views, width), f32),
        in_specs=[vmem, vmem],
        out_specs=vmem,
        scratch_shapes=[
            pltpu.VMEM((5, rows + 6, views, padded), f32),
            pltpu.VMEM((2, rows, width), f32),
            pltpu.VMEM((rows, 24, padded), f32),
            pltpu.VMEM((2, rows, views, width), f32),
            pltpu.VMEM((2, rows + 6, views, padded), f32),
            pltpu.VMEM((7, 3, rows + 6, views, width), f32),
            pltpu.SemaphoreType.DMA((copies,)),
            pltpu.SemaphoreType.DMA((copies,)),
        ],
        compiler_params=pltpu.CompilerParams(
            collective_id=0, has_side_effects=True, vmem_limit_bytes=48 * 1024 * 1024
        ),
    )(by_row, light_field)
    return refined.transpose(1, 0, 2)


def solution(mesh):
    spec = P("view", "row", None)
    return jax.shard_map(local, mesh=mesh, in_specs=(spec,), out_specs=spec, check_vma=False)
```

```python
import functools
import math

import jax
import jax.numpy as jnp
from jax import lax
from jax.experimental import pallas as pl
from jax.experimental.pallas import tpu as pltpu
from jax.sharding import PartitionSpec as P

DAMPING = 0.1
FLOOR = 0.05
LANES = 128
LOG2E = 1.4426950408889634
RANGE_SCALE = math.sqrt(LOG2E / 2.0)
MESH = pl.DeviceIdType.MESH


def moved(value, offset):
    if offset == 0:
        return value
    width = value.shape[-1]
    return pltpu.roll(value, (-offset) % width, value.ndim - 1)


def tensor_terms(space, angle):
    terms = []
    for left, right in ((space, space), (space, angle), (angle, angle)):
        a, b, c = (x * y for x, y in zip(left, right))
        terms.append((a + c) + 2.0 * b)
    return terms


def five(m2, m1, c0, p1, p2):
    return (m2 + p2) + 4.0 * (m1 + p1) + 6.0 * c0


def disparity_confidence(ss, sa, aa):
    disparity = -sa / (ss + DAMPING)
    spread = aa - ss
    total = aa + ss
    confidence = (spread * spread + 4.0 * sa * sa) / (total * total + DAMPING)
    return disparity, confidence


def kernel(parts, x_ref, xv_ref, out_ref, lum, pair, wide, horiz, mw, moved_ref, sums, *sems):
    n_row = lax.axis_size("row")
    n_u = lax.axis_size("view") // 2
    d = lax.axis_index("view")
    r = lax.axis_index("row")
    u = d // 2
    h = lax.rem(d, 2)
    rows, _, width = x_ref.shape
    padded = width + 2 * LANES
    chunks = len(parts)
    begin = [LANES * sum(parts[:c]) for c in range(chunks)]
    inner = slice(LANES, LANES + width)

    up = u < n_u - 1
    down = u > 0
    both = jnp.logical_and(up, down)
    row_up = r < n_row - 1
    row_down = r > 0
    always = d >= 0
    held = (down, up, always, u >= 2, u < n_u - 2)
    to_up = {"view": d + 2}
    to_down = {"view": d - 2}
    to_pair = {"view": d + 1 - 2 * h}
    to_row_up = {"row": r + 1}
    to_row_down = {"row": r - 1}

    send_sems, recv_sems = sems
    used = [0]

    def copy(src, dst, device, sends, receives):
        i = used[0]
        used[0] += 1
        c = pltpu.make_async_remote_copy(
            src_ref=src, dst_ref=dst, send_sem=send_sems.at[i], recv_sem=recv_sems.at[i],
            device_id=device, device_id_type=MESH,
        )
        return c, sends, receives

    def start(item):
        pl.when(item[1])(item[0].start)

    def arrived(item):
        pl.when(item[2])(item[0].wait_recv)

    def left(item):
        pl.when(item[1])(item[0].wait_send)

    barrier = pltpu.get_barrier_semaphore()
    peers = ((up, to_up), (down, to_down), (always, to_pair), (row_up, to_row_up), (row_down, to_row_down))
    count = jnp.int32(0)
    for cond, device in peers:
        @pl.when(cond)
        def _(device=device):
            pl.semaphore_signal(barrier, inc=1, device_id=device, device_id_type=MESH)
        count = count + cond.astype(jnp.int32)
    pl.semaphore_wait(barrier, count)

    slots = (3, 0, 2, 1, 4)
    own_rows = pl.ds(3, rows)

    def cols(c):
        return pl.ds(LANES + begin[c], LANES * parts[c])

    def row_pair(high, high_to, low, low_to):
        return copy(high, high_to, to_row_up, row_up, row_down), copy(low, low_to, to_row_down, row_down, row_up)

    near, far, near_edge, far_edge, merged_edge = {}, {}, {}, {}, {}
    pair_copy = copy(xv_ref.at[pl.ds(6 * (1 - h), 2)], pair, to_pair, always, always)
    all_cols = pl.ds(LANES, width)
    own_edge = row_pair(
        x_ref.at[pl.ds(rows - 3, 3)], lum.at[2, pl.ds(0, 3), :, all_cols],
        x_ref.at[pl.ds(0, 3)], lum.at[2, pl.ds(3 + rows, 3), :, all_cols],
    )
    all_copies = [pair_copy, *own_edge]
    for c in range(chunks):
        own = x_ref.at[:, :, pl.ds(begin[c], LANES * parts[c])]
        near[c] = (
            copy(own, lum.at[0, own_rows, :, cols(c)], to_up, up, down),
            copy(own, lum.at[1, own_rows, :, cols(c)], to_down, down, up),
        )
        far[c] = (
            copy(lum.at[0, own_rows, :, cols(c)], lum.at[3, own_rows, :, cols(c)], to_up, both, held[3]),
            copy(lum.at[1, own_rows, :, cols(c)], lum.at[4, own_rows, :, cols(c)], to_down, both, held[4]),
        )
        for edges, first, depth in ((near_edge, 0, 3), (far_edge, 3, 2)):
            two = pl.ds(first, 2)
            edges[c] = row_pair(
                lum.at[two, pl.ds(3 + rows - depth, depth), :, cols(c)], lum.at[two, pl.ds(3 - depth, depth), :, cols(c)],
                lum.at[two, pl.ds(3, depth), :, cols(c)], lum.at[two, pl.ds(3 + rows, depth), :, cols(c)],
            )
        merged_edge[c] = row_pair(
            mw.at[:, pl.ds(rows, 3), :, cols(c)], mw.at[:, pl.ds(0, 3), :, cols(c)],
            mw.at[:, pl.ds(3, 3), :, cols(c)], mw.at[:, pl.ds(3 + rows, 3), :, cols(c)],
        )
        all_copies += [*near[c], *far[c], *near_edge[c], *far_edge[c], *merged_edge[c]]

    start(pair_copy)
    for c in range(chunks):
        for item in near[c]:
            start(item)
    for e in own_edge:
        start(e)

    zero_pad = jnp.zeros((8, LANES), jnp.float32)

    @pl.loop(0, rows + 6)
    def _(i):
        for side in (0, LANES + width):
            lum[2, i, :, side:side + LANES] = zero_pad
            for j in range(2):
                mw[j, i, :, side:side + LANES] = zero_pad

    for k in (0, 1, 3, 4):
        @pl.when(jnp.logical_not(held[k]))
        def _(k=k):
            @pl.loop(3, 3 + rows)
            def _(i):
                lum[k, i] = jnp.zeros((8, padded), jnp.float32)

    for cond, first in ((jnp.logical_not(row_down), 0), (jnp.logical_not(row_up), 3 + rows)):
        @pl.when(cond)
        def _(first=first):
            for k in range(5):
                for i in range(first, first + 3):
                    lum[k, i] = jnp.zeros((8, padded), jnp.float32)
            for j in range(2):
                for i in range(first, first + 3):
                    mw[j, i] = jnp.zeros((8, padded), jnp.float32)

    for i in range(rows):
        lum[2, 3 + i, :, inner] = x_ref[i]
        wide[i, 8:16, inner] = x_ref[i]
        for side in (0, LANES + width):
            wide[i, :, side:side + LANES] = jnp.zeros((24, LANES), jnp.float32)
    arrived(pair_copy)
    for i in range(rows):
        for v in range(2):
            value = pair[v, i:i + 1, :]
            wide[i, 6 + v:7 + v, inner] = jnp.where(h == 1, value, 0.0)
            wide[i, 16 + v:17 + v, inner] = jnp.where(h == 0, value, 0.0)

    @pl.loop(0, rows)
    def _(i):
        views = [wide[i, 8 + o:16 + o, :] for o in (-2, -1, 0, 1, 2)]
        space = [moved(views[o], 1) - moved(views[o], -1) for o in (1, 2, 3)]
        angle = [views[o + 1] - views[o - 1] for o in (1, 2, 3)]
        ss, sa, aa = (
            five(*(moved(term, b) for b in (-2, -1, 0, 1, 2)))[:, inner] * (1.0 / 256.0)
            for term in tensor_terms(space, angle)
        )
        disparity, confidence = disparity_confidence(ss, sa, aa)
        horiz[0, i] = confidence * disparity
        horiz[1, i] = confidence

    for c in range(chunks):
        for item, on in zip(near[c], far[c]):
            arrived(item)
            start(on)
        for e in near_edge[c]:
            start(e)

    for e in own_edge:
        arrived(e)

    @pl.loop(0, rows + 6)
    def _(i):
        value = lum[2, i] * RANGE_SCALE
        for b in range(7):
            moved_ref[b, 0, i] = moved(value, b - 3)[:, inner]

    def vertical(c):
        @pl.loop(0, parts[c])
        def _(t):
            out_at = pl.multiple_of(begin[c] + t * LANES, LANES)
            at = pl.multiple_of(out_at + LANES, LANES)
            terms = []
            for i in range(1, rows + 5):
                space = [lum[k, i + 1, :, pl.ds(at, LANES)] - lum[k, i - 1, :, pl.ds(at, LANES)] for k in slots[1:4]]
                views = [lum[k, i, :, pl.ds(at, LANES)] for k in slots]
                angle = [views[o + 1] - views[o - 1] for o in (1, 2, 3)]
                terms.append(tensor_terms(space, angle))
            for i in range(rows):
                ss, sa, aa = (
                    five(*(terms[i + j][q] for j in range(5))) * (1.0 / 256.0) for q in range(3)
                )
                disparity, confidence = disparity_confidence(ss, sa, aa)
                product = horiz[0, i, :, pl.ds(out_at, LANES)]
                other = horiz[1, i, :, pl.ds(out_at, LANES)]
                total = other + confidence
                merged = (product + confidence * disparity) / (total + FLOOR)
                weight = FLOOR + 0.5 * total
                mw[0, 3 + i, :, pl.ds(at, LANES)] = merged * weight
                mw[1, 3 + i, :, pl.ds(at, LANES)] = weight

    def merge(c):
        for e in (*near_edge[c], *far_edge[c]):
            arrived(e)
        vertical(c)
        for e in merged_edge[c]:
            start(e)

    def refine(c, own):
        if not own:
            for e in merged_edge[c]:
                arrived(e)
        first = max(sum(parts[:c]) - 1, 0)
        last = sum(parts) if c == chunks - 1 else sum(parts[:c + 1]) - 1
        span = (last - first) * LANES

        def shift(i):
            for j in range(2):
                value = mw[j, i, :, first * LANES:last * LANES + 2 * LANES]
                for b in range(7):
                    moved_ref[b, 1 + j, i, :, first * LANES:last * LANES] = moved(value, b - 3)[:, LANES:LANES + span]

        for start_row, stop_row in ((3, 3 + rows),) if own else ((0, 3), (3 + rows, 6 + rows)):
            pl.loop(start_row, stop_row)(shift)
        used_rows = [i for i in range(rows + 6) if (3 <= i < 3 + rows) == own]

        @pl.loop(first, last)
        def _(t):
            at = pl.ds(pl.multiple_of(t * LANES, LANES), LANES)
            centre = [moved_ref[3, 0, 3 + i, :, at] for i in range(rows)]
            total = [None if own else sums[0, i, :, at] for i in range(rows)]
            norm = [None if own else sums[1, i, :, at] for i in range(rows)]
            for b in range(7):
                near_l = {i: moved_ref[b, 0, i, :, at] for i in used_rows}
                near_m = {i: moved_ref[b, 1, i, :, at] for i in used_rows}
                near_w = {i: moved_ref[b, 2, i, :, at] for i in used_rows}
                for i in range(rows):
                    for a in range(7):
                        if i + a not in used_rows:
                            continue
                        difference = near_l[i + a] - centre[i]
                        distance = ((a - 3) ** 2 + (b - 3) ** 2) / 8.0 * LOG2E
                        e = jnp.exp2(-distance - difference * difference)
                        m = e * near_m[i + a]
                        w = e * near_w[i + a]
                        total[i] = m if total[i] is None else total[i] + m
                        norm[i] = w if norm[i] is None else norm[i] + w
            for i in range(rows):
                if own:
                    sums[0, i, :, at] = total[i]
                    sums[1, i, :, at] = norm[i]
                else:
                    out_ref[i, :, at] = total[i] / norm[i]

    for c in range(chunks + 2):
        if c < chunks:
            for item in far[c]:
                arrived(item)
            for e in far_edge[c]:
                start(e)
        if 1 <= c <= chunks:
            merge(c - 1)
            if c == chunks and c >= 2:
                refine(c - 2, False)
            refine(c - 1, True)
        if 2 <= c != chunks:
            refine(c - 2, False)

    for item in all_copies:
        left(item)


def local(light_field):
    views, rows, width = light_field.shape
    tiles = width // LANES
    parts = (tiles - 2 * tiles // 5, 2 * tiles // 5)
    padded = width + 2 * LANES
    copies = 3 + len(parts) * 10
    f32 = jnp.float32
    by_row = light_field.transpose(1, 0, 2)
    vmem = pl.BlockSpec(memory_space=pltpu.VMEM)
    refined = pl.pallas_call(
        functools.partial(kernel, parts),
        out_shape=jax.ShapeDtypeStruct((rows, views, width), f32),
        in_specs=[vmem, vmem],
        out_specs=vmem,
        scratch_shapes=[
            pltpu.VMEM((5, rows + 6, views, padded), f32),
            pltpu.VMEM((2, rows, width), f32),
            pltpu.VMEM((rows, 24, padded), f32),
            pltpu.VMEM((2, rows, views, width), f32),
            pltpu.VMEM((2, rows + 6, views, padded), f32),
            pltpu.VMEM((7, 3, rows + 6, views, width), f32),
            pltpu.VMEM((2, rows, views, width), f32),
            pltpu.SemaphoreType.DMA((copies,)),
            pltpu.SemaphoreType.DMA((copies,)),
        ],
        compiler_params=pltpu.CompilerParams(
            collective_id=0, has_side_effects=True, vmem_limit_bytes=48 * 1024 * 1024
        ),
    )(by_row, light_field)
    return refined.transpose(1, 0, 2)


def solution(mesh):
    spec = P("view", "row", None)
    return jax.shard_map(local, mesh=mesh, in_specs=(spec,), out_specs=spec, check_vma=False)
```

```python
import functools
import math

import jax
import jax.numpy as jnp
from jax import lax
from jax.experimental import pallas as pl
from jax.experimental.pallas import tpu as pltpu
from jax.sharding import PartitionSpec as P

DAMPING = 0.1
FLOOR = 0.05
LANES = 128
LOG2E = 1.4426950408889634
RANGE_SCALE = math.sqrt(LOG2E / 2.0)
MESH = pl.DeviceIdType.MESH


def moved(value, offset):
    if offset == 0:
        return value
    width = value.shape[-1]
    return pltpu.roll(value, (-offset) % width, value.ndim - 1)


def tensor_terms(space, angle):
    terms = []
    for left, right in ((space, space), (space, angle), (angle, angle)):
        a, b, c = (x * y for x, y in zip(left, right))
        terms.append((a + c) + 2.0 * b)
    return terms


def five(m2, m1, c0, p1, p2):
    return (m2 + p2) + 4.0 * (m1 + p1) + 6.0 * c0


def disparity_confidence(ss, sa, aa):
    disparity = -sa / (ss + DAMPING)
    spread = aa - ss
    total = aa + ss
    confidence = (spread * spread + 4.0 * sa * sa) / (total * total + DAMPING)
    return disparity, confidence


def kernel(parts, x_ref, xv_ref, out_ref, lum, pair, wide, horiz, mw, moved_ref, closeness, sums, *sems):
    n_row = lax.axis_size("row")
    n_u = lax.axis_size("view") // 2
    d = lax.axis_index("view")
    r = lax.axis_index("row")
    u = d // 2
    h = lax.rem(d, 2)
    rows, _, width = x_ref.shape
    padded = width + 2 * LANES
    chunks = len(parts)
    begin = [LANES * sum(parts[:c]) for c in range(chunks)]
    inner = slice(LANES, LANES + width)

    up = u < n_u - 1
    down = u > 0
    both = jnp.logical_and(up, down)
    row_up = r < n_row - 1
    row_down = r > 0
    always = d >= 0
    held = (down, up, always, u >= 2, u < n_u - 2)
    to_up = {"view": d + 2}
    to_down = {"view": d - 2}
    to_pair = {"view": d + 1 - 2 * h}
    to_row_up = {"row": r + 1}
    to_row_down = {"row": r - 1}

    send_sems, recv_sems = sems
    used = [0]

    def copy(src, dst, device, sends, receives):
        i = used[0]
        used[0] += 1
        c = pltpu.make_async_remote_copy(
            src_ref=src, dst_ref=dst, send_sem=send_sems.at[i], recv_sem=recv_sems.at[i],
            device_id=device, device_id_type=MESH,
        )
        return c, sends, receives

    def start(item):
        pl.when(item[1])(item[0].start)

    def arrived(item):
        pl.when(item[2])(item[0].wait_recv)

    def left(item):
        pl.when(item[1])(item[0].wait_send)

    barrier = pltpu.get_barrier_semaphore()
    peers = ((up, to_up), (down, to_down), (always, to_pair), (row_up, to_row_up), (row_down, to_row_down))
    count = jnp.int32(0)
    for cond, device in peers:
        @pl.when(cond)
        def _(device=device):
            pl.semaphore_signal(barrier, inc=1, device_id=device, device_id_type=MESH)
        count = count + cond.astype(jnp.int32)
    pl.semaphore_wait(barrier, count)

    slots = (3, 0, 2, 1, 4)
    own_rows = pl.ds(3, rows)

    def cols(c):
        return pl.ds(LANES + begin[c], LANES * parts[c])

    def row_pair(high, high_to, low, low_to):
        return copy(high, high_to, to_row_up, row_up, row_down), copy(low, low_to, to_row_down, row_down, row_up)

    near, far, near_edge, far_edge, merged_edge = {}, {}, {}, {}, {}
    pair_copy = copy(xv_ref.at[pl.ds(6 * (1 - h), 2)], pair, to_pair, always, always)
    all_cols = pl.ds(LANES, width)
    own_edge = row_pair(
        x_ref.at[pl.ds(rows - 3, 3)], lum.at[2, pl.ds(0, 3), :, all_cols],
        x_ref.at[pl.ds(0, 3)], lum.at[2, pl.ds(3 + rows, 3), :, all_cols],
    )
    all_copies = [pair_copy, *own_edge]
    for c in range(chunks):
        own = x_ref.at[:, :, pl.ds(begin[c], LANES * parts[c])]
        near[c] = (
            copy(own, lum.at[0, own_rows, :, cols(c)], to_up, up, down),
            copy(own, lum.at[1, own_rows, :, cols(c)], to_down, down, up),
        )
        far[c] = (
            copy(lum.at[0, own_rows, :, cols(c)], lum.at[3, own_rows, :, cols(c)], to_up, both, held[3]),
            copy(lum.at[1, own_rows, :, cols(c)], lum.at[4, own_rows, :, cols(c)], to_down, both, held[4]),
        )
        for edges, first, depth in ((near_edge, 0, 3), (far_edge, 3, 2)):
            two = pl.ds(first, 2)
            edges[c] = row_pair(
                lum.at[two, pl.ds(3 + rows - depth, depth), :, cols(c)], lum.at[two, pl.ds(3 - depth, depth), :, cols(c)],
                lum.at[two, pl.ds(3, depth), :, cols(c)], lum.at[two, pl.ds(3 + rows, depth), :, cols(c)],
            )
        merged_edge[c] = row_pair(
            mw.at[:, pl.ds(rows, 3), :, cols(c)], mw.at[:, pl.ds(0, 3), :, cols(c)],
            mw.at[:, pl.ds(3, 3), :, cols(c)], mw.at[:, pl.ds(3 + rows, 3), :, cols(c)],
        )
        all_copies += [*near[c], *far[c], *near_edge[c], *far_edge[c], *merged_edge[c]]

    start(pair_copy)
    for c in range(chunks):
        for item in near[c]:
            start(item)
    for e in own_edge:
        start(e)

    zero_pad = jnp.zeros((8, LANES), jnp.float32)

    @pl.loop(0, rows + 6)
    def _(i):
        for side in (0, LANES + width):
            lum[2, i, :, side:side + LANES] = zero_pad
            for j in range(2):
                mw[j, i, :, side:side + LANES] = zero_pad

    for k in (0, 1, 3, 4):
        @pl.when(jnp.logical_not(held[k]))
        def _(k=k):
            @pl.loop(3, 3 + rows)
            def _(i):
                lum[k, i] = jnp.zeros((8, padded), jnp.float32)

    for cond, first in ((jnp.logical_not(row_down), 0), (jnp.logical_not(row_up), 3 + rows)):
        @pl.when(cond)
        def _(first=first):
            for k in range(5):
                for i in range(first, first + 3):
                    lum[k, i] = jnp.zeros((8, padded), jnp.float32)
            for j in range(2):
                for i in range(first, first + 3):
                    mw[j, i] = jnp.zeros((8, padded), jnp.float32)

    for i in range(rows):
        lum[2, 3 + i, :, inner] = x_ref[i]
        wide[i, 8:16, inner] = x_ref[i]
        for side in (0, LANES + width):
            wide[i, :, side:side + LANES] = jnp.zeros((24, LANES), jnp.float32)
    arrived(pair_copy)
    for i in range(rows):
        for v in range(2):
            value = pair[v, i:i + 1, :]
            wide[i, 6 + v:7 + v, inner] = jnp.where(h == 1, value, 0.0)
            wide[i, 16 + v:17 + v, inner] = jnp.where(h == 0, value, 0.0)

    @pl.loop(0, rows)
    def _(i):
        views = [wide[i, 8 + o:16 + o, :] for o in (-2, -1, 0, 1, 2)]
        space = [moved(views[o], 1) - moved(views[o], -1) for o in (1, 2, 3)]
        angle = [views[o + 1] - views[o - 1] for o in (1, 2, 3)]
        ss, sa, aa = (
            five(*(moved(term, b) for b in (-2, -1, 0, 1, 2)))[:, inner] * (1.0 / 256.0)
            for term in tensor_terms(space, angle)
        )
        disparity, confidence = disparity_confidence(ss, sa, aa)
        horiz[0, i] = confidence * disparity
        horiz[1, i] = confidence

    for c in range(chunks):
        for item, on in zip(near[c], far[c]):
            arrived(item)
            start(on)
        for e in near_edge[c]:
            start(e)

    for e in own_edge:
        arrived(e)

    @pl.loop(0, rows + 6)
    def _(i):
        value = lum[2, i] * RANGE_SCALE
        for b in range(7):
            moved_ref[b, 0, i] = moved(value, b - 3)[:, inner]

    @pl.loop(0, width // LANES)
    def _(t):
        at = pl.ds(pl.multiple_of(t * LANES, LANES), LANES)
        centre = [moved_ref[3, 0, 3 + i, :, at] for i in range(rows)]
        for b in range(7):
            near_l = [moved_ref[b, 0, i, :, at] for i in range(rows + 6)]
            for i in range(rows):
                for a in range(7):
                    difference = near_l[i + a] - centre[i]
                    distance = ((a - 3) ** 2 + (b - 3) ** 2) / 8.0 * LOG2E
                    closeness[7 * b + a, i, :, at] = jnp.exp2(-distance - difference * difference)

    def vertical(c):
        @pl.loop(0, parts[c])
        def _(t):
            out_at = pl.multiple_of(begin[c] + t * LANES, LANES)
            at = pl.multiple_of(out_at + LANES, LANES)
            terms = []
            for i in range(1, rows + 5):
                space = [lum[k, i + 1, :, pl.ds(at, LANES)] - lum[k, i - 1, :, pl.ds(at, LANES)] for k in slots[1:4]]
                views = [lum[k, i, :, pl.ds(at, LANES)] for k in slots]
                angle = [views[o + 1] - views[o - 1] for o in (1, 2, 3)]
                terms.append(tensor_terms(space, angle))
            for i in range(rows):
                ss, sa, aa = (
                    five(*(terms[i + j][q] for j in range(5))) * (1.0 / 256.0) for q in range(3)
                )
                disparity, confidence = disparity_confidence(ss, sa, aa)
                product = horiz[0, i, :, pl.ds(out_at, LANES)]
                other = horiz[1, i, :, pl.ds(out_at, LANES)]
                total = other + confidence
                merged = (product + confidence * disparity) / (total + FLOOR)
                weight = FLOOR + 0.5 * total
                mw[0, 3 + i, :, pl.ds(at, LANES)] = merged * weight
                mw[1, 3 + i, :, pl.ds(at, LANES)] = weight

    def merge(c):
        for e in (*near_edge[c], *far_edge[c]):
            arrived(e)
        vertical(c)
        for e in merged_edge[c]:
            start(e)

    def refine(c, own):
        if not own:
            for e in merged_edge[c]:
                arrived(e)
        first = max(sum(parts[:c]) - 1, 0)
        last = sum(parts) if c == chunks - 1 else sum(parts[:c + 1]) - 1
        span = (last - first) * LANES

        def shift(i):
            for j in range(2):
                value = mw[j, i, :, first * LANES:last * LANES + 2 * LANES]
                for b in range(7):
                    moved_ref[b, 1 + j, i, :, first * LANES:last * LANES] = moved(value, b - 3)[:, LANES:LANES + span]

        for start_row, stop_row in ((3, 3 + rows),) if own else ((0, 3), (3 + rows, 6 + rows)):
            pl.loop(start_row, stop_row)(shift)
        used_rows = [i for i in range(rows + 6) if (3 <= i < 3 + rows) == own]

        @pl.loop(first, last)
        def _(t):
            at = pl.ds(pl.multiple_of(t * LANES, LANES), LANES)
            total = [None if own else sums[0, i, :, at] for i in range(rows)]
            norm = [None if own else sums[1, i, :, at] for i in range(rows)]
            for b in range(7):
                near_m = {i: moved_ref[b, 1, i, :, at] for i in used_rows}
                near_w = {i: moved_ref[b, 2, i, :, at] for i in used_rows}
                for i in range(rows):
                    for a in range(7):
                        if i + a not in used_rows:
                            continue
                        e = closeness[7 * b + a, i, :, at]
                        m = e * near_m[i + a]
                        w = e * near_w[i + a]
                        total[i] = m if total[i] is None else total[i] + m
                        norm[i] = w if norm[i] is None else norm[i] + w
            for i in range(rows):
                if own:
                    sums[0, i, :, at] = total[i]
                    sums[1, i, :, at] = norm[i]
                else:
                    out_ref[i, :, at] = total[i] / norm[i]

    for c in range(chunks + 2):
        if c < chunks:
            for item in far[c]:
                arrived(item)
            for e in far_edge[c]:
                start(e)
        if 1 <= c <= chunks:
            merge(c - 1)
            if c == chunks and c >= 2:
                refine(c - 2, False)
            refine(c - 1, True)
        if 2 <= c != chunks:
            refine(c - 2, False)

    for item in all_copies:
        left(item)


def local(light_field):
    views, rows, width = light_field.shape
    tiles = width // LANES
    parts = (tiles - 2 * tiles // 5, 2 * tiles // 5)
    padded = width + 2 * LANES
    copies = 3 + len(parts) * 10
    f32 = jnp.float32
    by_row = light_field.transpose(1, 0, 2)
    vmem = pl.BlockSpec(memory_space=pltpu.VMEM)
    refined = pl.pallas_call(
        functools.partial(kernel, parts),
        out_shape=jax.ShapeDtypeStruct((rows, views, width), f32),
        in_specs=[vmem, vmem],
        out_specs=vmem,
        scratch_shapes=[
            pltpu.VMEM((5, rows + 6, views, padded), f32),
            pltpu.VMEM((2, rows, width), f32),
            pltpu.VMEM((rows, 24, padded), f32),
            pltpu.VMEM((2, rows, views, width), f32),
            pltpu.VMEM((2, rows + 6, views, padded), f32),
            pltpu.VMEM((7, 3, rows + 6, views, width), f32),
            pltpu.VMEM((49, rows, views, width), f32),
            pltpu.VMEM((2, rows, views, width), f32),
            pltpu.SemaphoreType.DMA((copies,)),
            pltpu.SemaphoreType.DMA((copies,)),
        ],
        compiler_params=pltpu.CompilerParams(
            collective_id=0, has_side_effects=True, vmem_limit_bytes=48 * 1024 * 1024
        ),
    )(by_row, light_field)
    return refined.transpose(1, 0, 2)


def solution(mesh):
    spec = P("view", "row", None)
    return jax.shard_map(local, mesh=mesh, in_specs=(spec,), out_specs=spec, check_vma=False)
```

```python
import functools
import math

import jax
import jax.numpy as jnp
from jax import lax
from jax.experimental import pallas as pl
from jax.experimental.pallas import tpu as pltpu
from jax.sharding import PartitionSpec as P

DAMPING = 0.1
FLOOR = 0.05
LANES = 128
LOG2E = 1.4426950408889634
RANGE_SCALE = math.sqrt(LOG2E / 2.0)
MESH = pl.DeviceIdType.MESH


def moved(value, offset):
    if offset == 0:
        return value
    width = value.shape[-1]
    return pltpu.roll(value, (-offset) % width, value.ndim - 1)


def tensor_terms(space, angle):
    terms = []
    for left, right in ((space, space), (space, angle), (angle, angle)):
        a, b, c = (x * y for x, y in zip(left, right))
        terms.append((a + c) + 2.0 * b)
    return terms


def five(m2, m1, c0, p1, p2):
    return (m2 + p2) + 4.0 * (m1 + p1) + 6.0 * c0


def disparity_confidence(ss, sa, aa):
    disparity = -sa / (ss + DAMPING)
    spread = aa - ss
    total = aa + ss
    confidence = (spread * spread + 4.0 * sa * sa) / (total * total + DAMPING)
    return disparity, confidence


def kernel(parts, x_ref, xv_ref, out_ref, lum, pair, wide, horiz, mw, moved_ref, closeness, sums, *sems):
    n_row = lax.axis_size("row")
    n_u = lax.axis_size("view") // 2
    d = lax.axis_index("view")
    r = lax.axis_index("row")
    u = d // 2
    h = lax.rem(d, 2)
    rows, _, width = x_ref.shape
    padded = width + 2 * LANES
    chunks = len(parts)
    begin = [LANES * sum(parts[:c]) for c in range(chunks)]
    inner = slice(LANES, LANES + width)

    up = u < n_u - 1
    down = u > 0
    both = jnp.logical_and(up, down)
    row_up = r < n_row - 1
    row_down = r > 0
    always = d >= 0
    low_half = r == n_row // 2 - 1
    high_half = r == n_row // 2
    middle = jnp.logical_or(low_half, high_half)
    halo = jnp.where(high_half, 1, 3 + rows)
    held = (down, up, always, u >= 2, u < n_u - 2)
    to_up = {"view": d + 2}
    to_down = {"view": d - 2}
    to_pair = {"view": d + 1 - 2 * h}
    to_row_up = {"row": r + 1}
    to_row_down = {"row": r - 1}

    send_sems, recv_sems = sems
    used = [0]

    def copy(src, dst, device, sends, receives):
        i = used[0]
        used[0] += 1
        c = pltpu.make_async_remote_copy(
            src_ref=src, dst_ref=dst, send_sem=send_sems.at[i], recv_sem=recv_sems.at[i],
            device_id=device, device_id_type=MESH,
        )
        return c, sends, receives

    def start(item):
        pl.when(item[1])(item[0].start)

    def arrived(item):
        pl.when(item[2])(item[0].wait_recv)

    def left(item):
        pl.when(item[1])(item[0].wait_send)

    barrier = pltpu.get_barrier_semaphore()
    peers = ((up, to_up), (down, to_down), (always, to_pair), (row_up, to_row_up), (row_down, to_row_down))
    count = jnp.int32(0)
    for cond, device in peers:
        @pl.when(cond)
        def _(device=device):
            pl.semaphore_signal(barrier, inc=1, device_id=device, device_id_type=MESH)
        count = count + cond.astype(jnp.int32)
    pl.semaphore_wait(barrier, count)

    slots = (3, 0, 2, 1, 4)
    own_rows = pl.ds(3, rows)

    def cols(c):
        return pl.ds(LANES + begin[c], LANES * parts[c])

    def row_pair(high, high_to, low, low_to):
        return copy(high, high_to, to_row_up, row_up, row_down), copy(low, low_to, to_row_down, row_down, row_up)

    def apart(edges):
        (high, high_sends, high_receives), (low, low_sends, low_receives) = edges
        not_low, not_high = jnp.logical_not(low_half), jnp.logical_not(high_half)
        return (
            (high, jnp.logical_and(high_sends, not_low), jnp.logical_and(high_receives, not_high)),
            (low, jnp.logical_and(low_sends, not_high), jnp.logical_and(low_receives, not_low)),
        )

    near, far, near_edge, far_edge, merged_edge, far_halo = {}, {}, {}, {}, {}, {}
    pair_copy = copy(xv_ref.at[pl.ds(6 * (1 - h), 2)], pair, to_pair, always, always)
    all_cols = pl.ds(LANES, width)
    own_edge = row_pair(
        x_ref.at[pl.ds(rows - 3, 3)], lum.at[2, pl.ds(0, 3), :, all_cols],
        x_ref.at[pl.ds(0, 3)], lum.at[2, pl.ds(3 + rows, 3), :, all_cols],
    )
    all_copies = [pair_copy, *own_edge]
    for c in range(chunks):
        own = x_ref.at[:, :, pl.ds(begin[c], LANES * parts[c])]
        near[c] = (
            copy(own, lum.at[0, own_rows, :, cols(c)], to_up, up, down),
            copy(own, lum.at[1, own_rows, :, cols(c)], to_down, down, up),
        )
        far[c] = (
            copy(lum.at[0, own_rows, :, cols(c)], lum.at[3, own_rows, :, cols(c)], to_up, both, held[3]),
            copy(lum.at[1, own_rows, :, cols(c)], lum.at[4, own_rows, :, cols(c)], to_down, both, held[4]),
        )
        for edges, first, depth in ((near_edge, 0, 3), (far_edge, 3, 2)):
            two = pl.ds(first, 2)
            edges[c] = row_pair(
                lum.at[two, pl.ds(3 + rows - depth, depth), :, cols(c)], lum.at[two, pl.ds(3 - depth, depth), :, cols(c)],
                lum.at[two, pl.ds(3, depth), :, cols(c)], lum.at[two, pl.ds(3 + rows, depth), :, cols(c)],
            )
        far_edge[c] = apart(far_edge[c])
        beside = pl.ds(halo, 2)
        far_halo[c] = (
            copy(lum.at[0, beside, :, cols(c)], lum.at[3, beside, :, cols(c)], to_up,
                 jnp.logical_and(both, middle), jnp.logical_and(held[3], middle)),
            copy(lum.at[1, beside, :, cols(c)], lum.at[4, beside, :, cols(c)], to_down,
                 jnp.logical_and(both, middle), jnp.logical_and(held[4], middle)),
        )
        merged_edge[c] = row_pair(
            mw.at[:, pl.ds(rows, 3), :, cols(c)], mw.at[:, pl.ds(0, 3), :, cols(c)],
            mw.at[:, pl.ds(3, 3), :, cols(c)], mw.at[:, pl.ds(3 + rows, 3), :, cols(c)],
        )
        all_copies += [*near[c], *far[c], *near_edge[c], *far_edge[c], *far_halo[c], *merged_edge[c]]

    start(pair_copy)
    for c in range(chunks):
        for item in near[c]:
            start(item)
    for e in own_edge:
        start(e)

    zero_pad = jnp.zeros((8, LANES), jnp.float32)

    @pl.loop(0, rows + 6)
    def _(i):
        for side in (0, LANES + width):
            lum[2, i, :, side:side + LANES] = zero_pad
            for j in range(2):
                mw[j, i, :, side:side + LANES] = zero_pad

    for k in (0, 1, 3, 4):
        @pl.when(jnp.logical_not(held[k]))
        def _(k=k):
            @pl.loop(3, 3 + rows)
            def _(i):
                lum[k, i] = jnp.zeros((8, padded), jnp.float32)

    for k in (3, 4):
        @pl.when(jnp.logical_and(jnp.logical_not(held[k]), middle))
        def _(k=k):
            for j in range(2):
                lum[k, halo + j] = jnp.zeros((8, padded), jnp.float32)

    for cond, first in ((jnp.logical_not(row_down), 0), (jnp.logical_not(row_up), 3 + rows)):
        @pl.when(cond)
        def _(first=first):
            for k in range(5):
                for i in range(first, first + 3):
                    lum[k, i] = jnp.zeros((8, padded), jnp.float32)
            for j in range(2):
                for i in range(first, first + 3):
                    mw[j, i] = jnp.zeros((8, padded), jnp.float32)

    for i in range(rows):
        lum[2, 3 + i, :, inner] = x_ref[i]
        wide[i, 8:16, inner] = x_ref[i]
        for side in (0, LANES + width):
            wide[i, :, side:side + LANES] = jnp.zeros((24, LANES), jnp.float32)
    arrived(pair_copy)
    for i in range(rows):
        for v in range(2):
            value = pair[v, i:i + 1, :]
            wide[i, 6 + v:7 + v, inner] = jnp.where(h == 1, value, 0.0)
            wide[i, 16 + v:17 + v, inner] = jnp.where(h == 0, value, 0.0)

    @pl.loop(0, rows)
    def _(i):
        views = [wide[i, 8 + o:16 + o, :] for o in (-2, -1, 0, 1, 2)]
        space = [moved(views[o], 1) - moved(views[o], -1) for o in (1, 2, 3)]
        angle = [views[o + 1] - views[o - 1] for o in (1, 2, 3)]
        ss, sa, aa = (
            five(*(moved(term, b) for b in (-2, -1, 0, 1, 2)))[:, inner] * (1.0 / 256.0)
            for term in tensor_terms(space, angle)
        )
        disparity, confidence = disparity_confidence(ss, sa, aa)
        horiz[0, i] = confidence * disparity
        horiz[1, i] = confidence

    for c in range(chunks):
        for item, on in zip(near[c], far[c]):
            arrived(item)
            start(on)
        for e in near_edge[c]:
            start(e)

    for e in own_edge:
        arrived(e)

    @pl.loop(0, rows + 6)
    def _(i):
        value = lum[2, i] * RANGE_SCALE
        for b in range(7):
            moved_ref[b, 0, i] = moved(value, b - 3)[:, inner]

    @pl.loop(0, width // LANES)
    def _(t):
        at = pl.ds(pl.multiple_of(t * LANES, LANES), LANES)
        centre = [moved_ref[3, 0, 3 + i, :, at] for i in range(rows)]
        for b in range(7):
            near_l = [moved_ref[b, 0, i, :, at] for i in range(rows + 6)]
            for i in range(rows):
                for a in range(7):
                    difference = near_l[i + a] - centre[i]
                    distance = ((a - 3) ** 2 + (b - 3) ** 2) / 8.0 * LOG2E
                    closeness[7 * b + a, i, :, at] = jnp.exp2(-distance - difference * difference)

    for c in range(chunks):
        pl.when(high_half)(near_edge[c][0][0].wait_recv)
        pl.when(low_half)(near_edge[c][1][0].wait_recv)
        for item in far_halo[c]:
            start(item)

    def vertical(c):
        @pl.loop(0, parts[c])
        def _(t):
            out_at = pl.multiple_of(begin[c] + t * LANES, LANES)
            at = pl.multiple_of(out_at + LANES, LANES)
            terms = []
            for i in range(1, rows + 5):
                space = [lum[k, i + 1, :, pl.ds(at, LANES)] - lum[k, i - 1, :, pl.ds(at, LANES)] for k in slots[1:4]]
                views = [lum[k, i, :, pl.ds(at, LANES)] for k in slots]
                angle = [views[o + 1] - views[o - 1] for o in (1, 2, 3)]
                terms.append(tensor_terms(space, angle))
            for i in range(rows):
                ss, sa, aa = (
                    five(*(terms[i + j][q] for j in range(5))) * (1.0 / 256.0) for q in range(3)
                )
                disparity, confidence = disparity_confidence(ss, sa, aa)
                product = horiz[0, i, :, pl.ds(out_at, LANES)]
                other = horiz[1, i, :, pl.ds(out_at, LANES)]
                total = other + confidence
                merged = (product + confidence * disparity) / (total + FLOOR)
                weight = FLOOR + 0.5 * total
                mw[0, 3 + i, :, pl.ds(at, LANES)] = merged * weight
                mw[1, 3 + i, :, pl.ds(at, LANES)] = weight

    def merge(c):
        for e in (*apart(near_edge[c]), *far_edge[c], *far_halo[c]):
            arrived(e)
        vertical(c)
        for e in merged_edge[c]:
            start(e)

    def refine(c, own):
        if not own:
            for e in merged_edge[c]:
                arrived(e)
        first = max(sum(parts[:c]) - 1, 0)
        last = sum(parts) if c == chunks - 1 else sum(parts[:c + 1]) - 1
        span = (last - first) * LANES

        def shift(i):
            for j in range(2):
                value = mw[j, i, :, first * LANES:last * LANES + 2 * LANES]
                for b in range(7):
                    moved_ref[b, 1 + j, i, :, first * LANES:last * LANES] = moved(value, b - 3)[:, LANES:LANES + span]

        for start_row, stop_row in ((3, 3 + rows),) if own else ((0, 3), (3 + rows, 6 + rows)):
            pl.loop(start_row, stop_row)(shift)
        used_rows = [i for i in range(rows + 6) if (3 <= i < 3 + rows) == own]

        @pl.loop(first, last)
        def _(t):
            at = pl.ds(pl.multiple_of(t * LANES, LANES), LANES)
            total = [None if own else sums[0, i, :, at] for i in range(rows)]
            norm = [None if own else sums[1, i, :, at] for i in range(rows)]
            for b in range(7):
                near_m = {i: moved_ref[b, 1, i, :, at] for i in used_rows}
                near_w = {i: moved_ref[b, 2, i, :, at] for i in used_rows}
                for i in range(rows):
                    for a in range(7):
                        if i + a not in used_rows:
                            continue
                        e = closeness[7 * b + a, i, :, at]
                        m = e * near_m[i + a]
                        w = e * near_w[i + a]
                        total[i] = m if total[i] is None else total[i] + m
                        norm[i] = w if norm[i] is None else norm[i] + w
            for i in range(rows):
                if own:
                    sums[0, i, :, at] = total[i]
                    sums[1, i, :, at] = norm[i]
                else:
                    out_ref[i, :, at] = total[i] / norm[i]

    for c in range(chunks + 2):
        if c < chunks:
            for item in far[c]:
                arrived(item)
            for e in far_edge[c]:
                start(e)
        if 1 <= c <= chunks:
            merge(c - 1)
            if c == chunks and c >= 2:
                refine(c - 2, False)
            refine(c - 1, True)
        if 2 <= c != chunks:
            refine(c - 2, False)

    for item in all_copies:
        left(item)


def local(light_field):
    views, rows, width = light_field.shape
    tiles = width // LANES
    parts = (tiles - 2 * tiles // 5, 2 * tiles // 5)
    padded = width + 2 * LANES
    copies = 3 + len(parts) * 12
    f32 = jnp.float32
    by_row = light_field.transpose(1, 0, 2)
    vmem = pl.BlockSpec(memory_space=pltpu.VMEM)
    refined = pl.pallas_call(
        functools.partial(kernel, parts),
        out_shape=jax.ShapeDtypeStruct((rows, views, width), f32),
        in_specs=[vmem, vmem],
        out_specs=vmem,
        scratch_shapes=[
            pltpu.VMEM((5, rows + 6, views, padded), f32),
            pltpu.VMEM((2, rows, width), f32),
            pltpu.VMEM((rows, 24, padded), f32),
            pltpu.VMEM((2, rows, views, width), f32),
            pltpu.VMEM((2, rows + 6, views, padded), f32),
            pltpu.VMEM((7, 3, rows + 6, views, width), f32),
            pltpu.VMEM((49, rows, views, width), f32),
            pltpu.VMEM((2, rows, views, width), f32),
            pltpu.SemaphoreType.DMA((copies,)),
            pltpu.SemaphoreType.DMA((copies,)),
        ],
        compiler_params=pltpu.CompilerParams(
            collective_id=0, has_side_effects=True, vmem_limit_bytes=48 * 1024 * 1024
        ),
    )(by_row, light_field)
    return refined.transpose(1, 0, 2)


def solution(mesh):
    spec = P("view", "row", None)
    return jax.shard_map(local, mesh=mesh, in_specs=(spec,), out_specs=spec, check_vma=False)
```
